512 devices in a mesh: grp: 16 (over z_lo, core), dev: 32 (over z_hi, x, y).
Axes of the slice: x: 4, y: 4, z: 16 (z_hi: 2, z_lo: 8; z = z_hi * 8 + z_lo), core: 2. Of those that a mesh axis runs over, the one named last changes fastest.
Arguments:
- records: bfloat16 [2048, 4, 2048], P(('grp', 'dev')), may hold values from -6 to 6
- usable: int32 [2048, 4], replicated, may hold values 0 or 1
- panel_ids: int32 [2], replicated, may hold values from 0 to 31
Outputs:
- xcorr: bfloat16 [2, 64, 2048, 512], P(None, None, ('grp', 'dev'))
The draws below stay inside these ranges and needn't reach their ends.
Inputs may be any that keep to these rules, and one draw needn't show every extreme that they name: `panel_ids`: each entry names a panel.
All inputs are finite; a program needn't handle non-finite values.
Results may differ from the reference program's by a relative error of at most 0.0075.
Values may be sent and summed in bfloat16 or wider, within the bound.
A program may use at most 64 MiB of HBM per device.

```python
import math
import jax
import jax.numpy as jnp
from jax import lax

L = 2048
NF = 1024
SMOOTH = 64
NLAG = 512
WINS = 4
CH_DEV = 4
SRC_DEV = 2
STEPS = 2
NPANEL = 32
CHANNELS = 2048
N_GRP = 16
N_DEV = 32


def plant(array, stream_key, least, largest):
    longest = array.shape.index(max(array.shape))
    spots = []
    for shift in (0, 1):
        where = [jax.random.randint(jax.random.fold_in(stream_key, axis), (), 0, length) for axis, length in enumerate(array.shape)]
        where[longest] = (where[longest] + shift) % array.shape[longest]
        spots.append(tuple(where))
    return array.at[spots[0]].set(least).at[spots[1]].set(largest)


def block_levels(key, dims, cuts, smallest, largest):
    def one(axis_at, blocks):
        steps = jax.random.uniform(jax.random.fold_in(jax.random.fold_in(key, 6), axis_at), (blocks,), jnp.float32, smallest / len(cuts), largest / len(cuts))
        return jnp.repeat(jnp.exp(steps), dims[axis_at] // blocks).reshape((-1,) + (1,) * (len(dims) - axis_at - 1))

    loudness = one(*cuts[0])
    for cut in cuts[1:]:
        loudness = loudness * one(*cut)
    return loudness


def normal_values(key, shape, deviation, reach, split=(), kind=jnp.bfloat16):
    values = jax.random.normal(key, shape, jnp.float32) * deviation
    if len(split) > 0:
        values = block_levels(key, shape, split, -0.22, 0.18) * values
    return jnp.clip(values, min=-reach, max=reach).astype(kind)


def setup_inputs(seed: int = 0) -> dict:
    splits = jax.random.split(jax.random.key(seed), 4)
    return {
        "records": normal_values(splits[0], (CHANNELS, WINS, L), 1.0, 6.0, ((0, 512),)),
        "usable": plant((jax.random.randint(splits[1], (CHANNELS, WINS), 0, 4) < 3).astype(jnp.int32), jax.random.fold_in(splits[1], 1), 0, 1),
        "panel_ids": jax.random.randint(splits[2], (STEPS,), 0, NPANEL).astype(jnp.int32),
    }


def forward_table(length, bin_count):
    samples = jnp.arange(length, dtype=jnp.int32)[:, None]
    bin_index = jnp.arange(1, bin_count + 1, dtype=jnp.int32)[None, :]
    phases = 2.0 * math.pi / length * (samples * bin_index % length).astype(jnp.float32)
    return jnp.concatenate([jnp.cos(phases), -jnp.sin(phases)], axis=1).astype(jnp.bfloat16)

def lag_table(length, bin_count, lag_count):
    bin_index = jnp.arange(1, bin_count + 1, dtype=jnp.int32)[:, None]
    lag_index = jnp.arange(lag_count, dtype=jnp.int32)[None, :] - lag_count // 2
    phases = 2.0 * math.pi / length * (bin_index * lag_index % length).astype(jnp.float32)
    factor = 1.0 / math.sqrt(bin_count)
    return jnp.concatenate([jnp.cos(phases) * factor, -jnp.sin(phases) * factor], axis=0).astype(jnp.bfloat16)

def band_matrix(bin_count, radius):
    positions = jnp.arange(bin_count, dtype=jnp.int32)
    nearby = jnp.abs(positions[:, None] - positions[None, :]) <= radius
    return nearby.astype(jnp.float32) / (2 * radius + 1)

def whiten(records, bin_count, radius):
    row_count, windows, length = records.shape
    flattened = records.reshape(row_count * windows, length)
    spectra = jnp.dot(flattened, forward_table(length, bin_count), preferred_element_type=jnp.float32)
    real_part = spectra[:, :bin_count]
    imag_part = spectra[:, bin_count:]
    amplitude = jnp.sqrt(real_part * real_part + imag_part * imag_part)
    smooth = jnp.dot(amplitude, band_matrix(bin_count, radius), precision=lax.Precision.HIGHEST)
    whitened = spectra / (jnp.concatenate([smooth, smooth], axis=1) + 1e-06)
    return whitened.astype(jnp.bfloat16).reshape(row_count, windows, 2 * bin_count)

def paired(left, right):
    return jnp.einsum('swf,rwf->srf', left.astype(jnp.float32), right.astype(jnp.float32))

def cross_spectra(sources, source_mask, receivers, receiver_mask, ltable, bin_count):
    source_re = sources[:, :, :bin_count]
    source_im = sources[:, :, bin_count:]
    recv_re = receivers[:, :, :bin_count]
    recv_im = receivers[:, :, bin_count:]
    real_sum = paired(source_re, recv_re) + paired(source_im, recv_im)
    imag_sum = paired(source_im, recv_re) - paired(source_re, recv_im)
    counts = jnp.dot(source_mask, receiver_mask.T, precision=lax.Precision.HIGHEST)
    denom = jnp.maximum(counts, 1.0)[:, :, None]
    stacked = jnp.concatenate([real_sum / denom, imag_sum / denom], axis=2).astype(jnp.bfloat16)
    source_count = sources.shape[0]
    recv_count = receivers.shape[0]
    lagged = jnp.dot(stacked.reshape(source_count * recv_count, 2 * bin_count), ltable, preferred_element_type=jnp.float32)
    return lagged.reshape(source_count, recv_count, ltable.shape[1]).astype(jnp.bfloat16)

def reference(records, usable, panel_ids):
    halves = CH_DEV // SRC_DEV
    whitened = whiten(records, NF, SMOOTH)
    masked = whitened * usable.astype(jnp.bfloat16)[:, :, None]
    mask_float = usable.astype(jnp.float32)
    grouped = masked.reshape(N_GRP, N_DEV, halves, SRC_DEV, WINS, 2 * NF)
    grouped_mask = mask_float.reshape(N_GRP, N_DEV, halves, SRC_DEV, WINS)
    recv_blocks = masked.reshape(N_GRP, N_DEV * CH_DEV, WINS, 2 * NF)
    mask_blocks = mask_float.reshape(N_GRP, N_DEV * CH_DEV, WINS)
    ltable = lag_table(L, NF, NLAG)
    results = []
    for step_index in range(STEPS):
        chosen = panel_ids[step_index]
        owning = chosen // halves
        within = chosen % halves
        sources = grouped[owning][:, within].reshape(N_DEV * SRC_DEV, WINS, 2 * NF)
        source_mask = grouped_mask[owning][:, within].reshape(N_DEV * SRC_DEV, WINS)

        def one_block(pieces):
            return cross_spectra(sources, source_mask, pieces[0], pieces[1], ltable, NF)
        mapped = lax.map(one_block, (recv_blocks, mask_blocks))
        results.append(jnp.transpose(mapped, (1, 0, 2, 3)).reshape(N_DEV * SRC_DEV, CHANNELS, NLAG))
    return jnp.stack(results)
```

```python
import math

import jax
import jax.numpy as jnp
import ml_dtypes
import numpy as np
from jax import lax
from jax.experimental import pallas as pl
from jax.experimental.pallas import tpu as pltpu
from jax.sharding import PartitionSpec as P

L = 2048
NF = 1024
RADIUS = 64
NLAG = 512
F32 = jnp.float32
BF16 = jnp.bfloat16
MESH = pl.DeviceIdType.MESH


def bins_of():
    lane = np.arange(128)
    bins = np.zeros((8, 128), np.int64)
    bins[0] = np.where(lane < 64, 16 * lane + 8, 16 * (lane - 63))
    for r in range(1, 8):
        bins[r] = 16 * lane + r
    return bins


def split_table(table):
    high = table.astype(ml_dtypes.bfloat16)
    low = (table - high.astype(np.float64)).astype(ml_dtypes.bfloat16)
    return high, low


def make_tables():
    bins = bins_of()
    natural = np.where(bins > NF, L - bins, bins)
    b = np.arange(128)
    angle = 2 * np.pi * np.outer(b, b) / 128
    cos, sin = np.cos(angle), np.sin(angle)
    dft = np.block([[cos, -sin], [sin, cos]])
    special = np.zeros((384, 256))
    for lane in range(64):
        special[128:256, lane] = cos[:, lane]
        special[256:384, lane] = sin[:, lane]
        special[128:256, 128 + lane] = -sin[:, lane]
        special[256:384, 128 + lane] = cos[:, lane]
    for lane in range(64, 128):
        special[0:128, lane] = np.cos(2 * np.pi * b * (lane - 63) / 128)
        special[0:128, 128 + lane] = -np.sin(2 * np.pi * b * (lane - 63) / 128)
    r = np.arange(16)[:, None]
    twiddle = 2 * np.pi * r * b[None, :] / L
    turn = np.stack([np.cos(twiddle), np.sin(twiddle)]).astype(np.float32)

    def near(left, right):
        return (np.abs(natural[left][:, None] - natural[right][None, :]) <= RADIUS).astype(np.float64)

    band = np.concatenate([near(1, 2), near(2, 2), near(3, 2), near(0, 2)], axis=0)
    band0 = np.concatenate([near(1, 0), near(0, 0)], axis=0)
    lag = np.arange(NLAG) - NLAG // 2
    phase = 2 * np.pi * ((bins.reshape(-1)[:, None] * lag[None, :]) % L) / L
    ltable = np.concatenate([np.cos(phase), -np.sin(phase)], axis=0) / math.sqrt(NF)
    bf = ml_dtypes.bfloat16
    bands = np.concatenate([np.concatenate([band[:256], band[256:]], axis=1), np.concatenate([band0[:128], band0[128:]], axis=1)], axis=0)
    packed = np.concatenate([*split_table(dft), *split_table(special), bands.astype(bf)], axis=0)
    return packed, turn, ltable.astype(bf)


def split(values):
    high = values.astype(BF16)
    return high, (values - high.astype(F32)).astype(BF16)


def dot(left, right):
    return jnp.dot(left, right, preferred_element_type=F32)


def transform(rows, tab_ref, turn_ref):
    count = rows.shape[0]
    x = [rows[:, 128 * a : 128 * a + 128] for a in range(16)]
    even = [None] + [x[a] + x[16 - a] for a in range(1, 8)]
    odd = [None] + [x[a] - x[16 - a] for a in range(1, 8)]
    parts_re, parts_im = [], []
    for r in range(9):
        re = x[0] + x[8] if r % 2 == 0 else x[0] - x[8]
        im = None
        for a in range(1, 8):
            c = math.cos(2 * math.pi * ((a * r) % 16) / 16)
            s = math.sin(2 * math.pi * ((a * r) % 16) / 16)
            if abs(c) > 1e-9:
                re = re + even[a] * c
            if abs(s) > 1e-9:
                im = odd[a] * -s if im is None else im + odd[a] * -s
        parts_re.append(re)
        parts_im.append(im)
    turned = []
    for r in range(1, 8):
        c, s = turn_ref[0, r : r + 1, :], turn_ref[1, r : r + 1, :]
        turned.append(jnp.concatenate([parts_re[r] * c + parts_im[r] * s, parts_im[r] * c - parts_re[r] * s], axis=1))
    y = jnp.concatenate(turned, axis=0)
    c, s = turn_ref[0, 8:9, :], turn_ref[1, 8:9, :]
    y0 = jnp.concatenate([parts_re[0], parts_re[8] * c, -(parts_re[8] * s)], axis=1)

    def product(values, at):
        high, low = split(values)
        n, depth = values.shape
        both = dot(jnp.concatenate([high, low], axis=0), tab_ref[at : at + depth])
        return both[:n] + both[n:] + dot(high, tab_ref[at + depth : at + 2 * depth])

    spectra = product(y, 0)
    spectra0 = product(y0, 512)
    re = [spectra0[:, :128]] + [spectra[count * j : count * j + count, :128] for j in range(7)]
    im = [spectra0[:, 128:]] + [spectra[count * j : count * j + count, 128:] for j in range(7)]
    return re, im


def running_mean(amplitude, tab_ref):
    count = amplitude[0].shape[0]
    below = [None, jnp.zeros_like(amplitude[0])]
    for r in range(2, 9):
        below.append(below[r - 1] + amplitude[r - 1])
    total = below[8]
    left = jnp.concatenate(
        [
            jnp.concatenate([below[r], amplitude[r], total - below[r] - amplitude[r], amplitude[0]], axis=1)
            for r in range(1, 8)
        ],
        axis=0,
    )
    left0 = jnp.concatenate([total, amplitude[0]], axis=1)

    def product(values, at):
        high, low = split(values)
        half = values.shape[1] // 2
        both = jnp.concatenate([high, low], axis=0)
        both = dot(both[:, :half], tab_ref[at : at + half, :128]) + dot(both[:, half:], tab_ref[at : at + half, 128:])
        return both[: values.shape[0]] + both[values.shape[0] :]

    sums = product(left, 1280)
    sums0 = product(left0, 1536)
    scale = 1.0 / (2 * RADIUS + 1)
    return [sums0 * scale] + [sums[count * j : count * j + count] * scale for j in range(7)]


def kernel(
    panel_ids_ref,
    x_hbm,
    usable_hbm,
    tab_hbm,
    turn_hbm,
    lt_hbm,
    out_ref,
    x_ref,
    usable_ref,
    tab_ref,
    turn_ref,
    units,
    picks,
    panel,
    own,
    other,
    recv,
    lhs,
    lt_ref,
    scales,
    outbox,
    in_sem,
    unit_send,
    unit_recv,
    other_send,
    other_recv,
    line_send,
    line_recv,
    plane_send,
    plane_recv,
    out_send,
    out_recv,
):
    g = lax.axis_index("grp")
    d = lax.axis_index("dev")
    z_lo, c = g // 2, g % 2
    z_hi, xx, yy = d // 16, (d // 4) % 4, d % 4
    mate = z_lo * 2 + (1 - c)

    loads = [
        pltpu.make_async_copy(source, target, in_sem.at[n])
        for n, (source, target) in enumerate(
            [(x_hbm, x_ref), (turn_hbm, turn_ref), (tab_hbm, tab_ref), (usable_hbm, usable_ref), (lt_hbm, lt_ref)]
        )
    ]
    for load in loads:
        load.start()

    barrier = pltpu.get_barrier_semaphore()

    def hello(grp, dev):
        pl.semaphore_signal(barrier, inc=1, device_id=(grp, dev), device_id_type=MESH)

    def hello_grp(k, carry):
        hello((g + k) % 16, d)
        return carry

    lax.fori_loop(1, 16, hello_grp, 0)

    def hello_line(k, carry):
        hello(2 * k + c, (1 - z_hi) * 16 + d % 16)
        return carry

    lax.fori_loop(0, 8, hello_line, 0)

    def hello_plane(k, carry):
        hello(g, z_hi * 16 + ((xx + k) % 4) * 4 + yy)
        hello(g, z_hi * 16 + xx * 4 + (yy + k) % 4)
        return carry

    lax.fori_loop(1, 4, hello_plane, 0)

    for load in loads[:4]:
        load.wait()
    rows = jnp.concatenate([x_ref[ch].astype(F32) for ch in range(4)], axis=0)
    spec_re, spec_im = transform(rows, tab_ref, turn_ref)
    amplitude = [jnp.sqrt(re * re + im * im) for re, im in zip(spec_re, spec_im)]
    smooth = running_mean(amplitude, tab_ref)

    lane16 = lax.broadcasted_iota(jnp.int32, (16, 128), 1)
    row16 = lax.broadcasted_iota(jnp.int32, (16, 128), 0)

    def mask_of(group):
        block = usable_ref[:, pl.ds(pl.multiple_of(group * 128, 128), 128)].astype(F32)
        tiled = jnp.concatenate([block] * 4, axis=0)
        chosen = jnp.where(lane16 == 4 * d + row16 // 4, tiled, 0.0)
        return jnp.sum(chosen, axis=1, keepdims=True)

    own_mask = mask_of(g)
    mate_mask = mask_of(mate)

    upper = [(jnp.full((8, 128), panel_ids_ref[t]) & 1) == 1 for t in range(2)]
    for k in range(8):
        inverse = 1.0 / (smooth[k] + 1e-06)
        re = (spec_re[k] * inverse).astype(BF16).astype(F32) * own_mask
        im = (spec_im[k] * inverse).astype(BF16).astype(F32) * own_mask
        own[k] = re.astype(BF16)
        own[8 + k] = im.astype(BF16)
        for t in range(2):
            pair = jnp.concatenate(
                [jnp.where(upper[t], re[8:], re[:8]), jnp.where(upper[t], im[8:], im[:8])], axis=0
            )
            units[2 * k + t] = pair.astype(BF16)

    pl.semaphore_wait(barrier, 29)

    def send_unit(k, carry):
        to = (g + k) % 16
        pltpu.make_async_remote_copy(
            src_ref=units.at[to],
            dst_ref=picks.at[g],
            send_sem=unit_send,
            recv_sem=unit_recv,
            device_id=(to, d),
            device_id_type=MESH,
        ).start()
        return carry

    lax.fori_loop(1, 16, send_unit, 0)
    to_mate = pltpu.make_async_remote_copy(
        src_ref=own,
        dst_ref=other,
        send_sem=other_send,
        recv_sem=other_recv,
        device_id=(mate, d),
        device_id_type=MESH,
    )
    to_mate.start()
    picks[g] = units[g]

    pltpu.make_async_copy(picks.at[pl.ds(0, 15)], picks.at[pl.ds(0, 15)], unit_recv).wait()
    chosen = panel_ids_ref[c]
    owner = jnp.full((16, 128), chosen) >> 1
    pick = jnp.where(owner == 0, picks[0].astype(F32), 0.0)
    for k in range(1, 16):
        pick = jnp.where(owner == k, picks[k].astype(F32), pick)
    panel[xx, yy, z_hi, z_lo] = pick.astype(BF16)

    mine = panel.at[xx, yy, z_hi, z_lo]

    def send_line(k, carry):
        z = (z_hi * 8 + z_lo + k) % 16
        pltpu.make_async_remote_copy(
            src_ref=mine,
            dst_ref=mine,
            send_sem=line_send,
            recv_sem=line_recv,
            device_id=((z % 8) * 2 + c, (z // 8) * 16 + d % 16),
            device_id_type=MESH,
        ).start()
        return carry

    lax.fori_loop(1, 16, send_line, 0)

    low = lax.broadcasted_iota(jnp.int32, (8, 128), 0) < 4

    def spread(side, source):
        def one(p, carry):
            tile = source[p].astype(F32)
            for pair in range(2):
                rows8 = tile[8 * pair : 8 * pair + 8]
                turned = pltpu.roll(rows8, 4, 0)
                recv[side, p, 2 * pair] = jnp.where(low, rows8, turned)
                recv[side, p, 2 * pair + 1] = jnp.where(low, turned, rows8)
            return carry

        lax.fori_loop(0, 16, one, 0)

    spread(0, own)
    to_mate.wait_recv()
    spread(1, other)

    block = usable_ref[:, :128]
    for k in range(1, 16):
        block = jnp.where(owner[:4] == k, usable_ref[:, 128 * k : 128 * k + 128], block)
    block = block.astype(F32)
    weights = jnp.concatenate([block] * 8, axis=0) * jnp.concatenate([own_mask, mate_mask], axis=0)
    row = lax.broadcasted_iota(jnp.int32, (512, 128), 0)
    lane = lax.broadcasted_iota(jnp.int32, (512, 128), 1)
    at_x = (xx + row // 128) % 4
    at_y = (yy + (row // 32) % 4) % 4
    at_dev = ((row // 16) % 2) * 16 + at_x * 4 + at_y
    half = jnp.full((512, 128), chosen) & 1
    picked = jnp.where(lane == at_dev * 4 + half * 2 + (row // 4) % 2, 1.0, 0.0).astype(BF16)
    counts = lax.dot_general(picked, weights.astype(BF16), (((1,), (1,)), ((), ())), preferred_element_type=F32)
    row32 = lax.broadcasted_iota(jnp.int32, (512, 32), 0)
    lane32 = lax.broadcasted_iota(jnp.int32, (512, 32), 1)
    match = lane32 // 4 == ((row32 // 8) % 2) * 4 + row32 % 4
    count = jnp.sum(jnp.where(match, counts, 0.0), axis=1, keepdims=True)
    scales[...] = jnp.broadcast_to(1.0 / jnp.maximum(count, 1.0), (512, 128))

    pltpu.make_async_copy(picks.at[pl.ds(0, 15)], picks.at[pl.ds(0, 15)], line_recv).wait()

    def send_block(h, bx, by, tx, ty):
        pltpu.make_async_remote_copy(
            src_ref=panel.at[bx, by, h],
            dst_ref=panel.at[bx, by, h],
            send_sem=plane_send,
            recv_sem=plane_recv.at[h, bx, by],
            device_id=(g, z_hi * 16 + tx * 4 + ty),
            device_id_type=MESH,
        ).start()

    def wait_block(h, bx, by):
        ref = panel.at[bx, by, h]
        pltpu.make_async_copy(ref, ref, plane_recv.at[h, bx, by]).wait()

    def send_first(k, carry):
        send_block(0, xx, yy, (xx + k) % 4, yy)
        send_block(1, xx, yy, xx, (yy + k) % 4)
        return carry

    def send_own(k, carry):
        send_block(0, xx, yy, xx, (yy + k) % 4)
        send_block(1, xx, yy, (xx + k) % 4, yy)
        return carry

    lax.fori_loop(1, 4, send_first, 0)
    lax.fori_loop(1, 4, send_own, 0)

    def forward(k, carry):
        bx, by = (xx + k) % 4, (yy + k) % 4
        wait_block(0, bx, yy)

        def on_y(m, inner):
            send_block(0, bx, yy, xx, (yy + m) % 4)
            return inner

        lax.fori_loop(1, 4, on_y, 0)
        wait_block(1, xx, by)

        def on_x(m, inner):
            send_block(1, xx, by, (xx + m) % 4, yy)
            return inner

        lax.fori_loop(1, 4, on_x, 0)
        return carry

    lax.fori_loop(1, 4, forward, 0)

    wait_block(1, (xx + 1) % 4, yy)
    wait_block(1, (xx + 2) % 4, yy)
    wait_block(1, (xx + 3) % 4, yy)
    wait_block(0, xx, (yy + 1) % 4)
    wait_block(0, xx, (yy + 2) % 4)
    wait_block(0, xx, (yy + 3) % 4)
    loads[4].wait()

    sub = lax.broadcasted_iota(jnp.int32, (8, 128), 0)
    even1 = sub % 2 == 0
    even2 = (sub // 2) % 2 == 0

    def fold(v):
        first = jnp.where(even1, v[0] + pltpu.roll(v[0], 7, 0), v[1] + pltpu.roll(v[1], 1, 0))
        second = jnp.where(even1, v[2] + pltpu.roll(v[2], 7, 0), v[3] + pltpu.roll(v[3], 1, 0))
        return jnp.where(even2, first + pltpu.roll(first, 6, 0), second + pltpu.roll(second, 2, 0))

    def cross(line, bx, by, h):
        slot = line * 2 + h
        for k in range(8):
            both = panel[bx, by, h, k].astype(F32)
            a, b = both[:8], both[8:]
            re_rows, im_rows = [], []
            for side in range(2):
                re, im = [], []
                for r in range(4):
                    cc, ee = recv[side, k, r], recv[side, 8 + k, r]
                    re.append(a * cc + b * ee)
                    im.append(b * cc - a * ee)
                re_rows.append(fold(re))
                im_rows.append(fold(im))
            at = pl.ds(pl.multiple_of(slot * 16, 16), 16)
            lhs[at, 128 * k : 128 * k + 128] = jnp.concatenate(re_rows, axis=0).astype(BF16)
            lhs[at, 1024 + 128 * k : 1152 + 128 * k] = jnp.concatenate(im_rows, axis=0).astype(BF16)

    def quarter(q, carry):
        bx = (xx + q) % 4

        def one_line(m, inner):
            by = (yy + m) % 4
            cross(q * 4 + m, bx, by, 0)
            cross(q * 4 + m, bx, by, 1)
            return inner

        lax.fori_loop(0, 4, one_line, 0)
        at = pl.ds(pl.multiple_of(q * 128, 128), 128)
        lagged = dot(lhs[at, :], lt_ref[...]) * jnp.concatenate([scales[at, :]] * 4, axis=1)
        for m in range(4):
            by = (yy + m) % 4
            for h in range(2):
                base = m * 32 + h * 16
                s = (h * 16 + bx * 4 + by) * 2
                for i in range(2):
                    out_ref[c, s + i] = lagged[base + 4 * i : base + 4 * i + 4].astype(BF16)
                    outbox[s + i] = lagged[base + 8 + 4 * i : base + 12 + 4 * i].astype(BF16)
        return carry

    quarter(0, 0)

    def later(q, carry):
        bx = (xx + q) % 4

        def wait_line(m, inner):
            by = (yy + m) % 4
            wait_block(0, bx, by)
            wait_block(1, bx, by)
            return inner

        lax.fori_loop(1, 4, wait_line, 0)
        return quarter(q, carry)

    lax.fori_loop(1, 4, later, 0)

    to_out = pltpu.make_async_remote_copy(
        src_ref=outbox,
        dst_ref=out_ref.at[c],
        send_sem=out_send,
        recv_sem=out_recv,
        device_id=(mate, d),
        device_id_type=MESH,
    )
    to_out.start()

    pltpu.make_async_copy(picks.at[pl.ds(0, 15)], picks.at[pl.ds(0, 15)], unit_send).wait()
    pltpu.make_async_copy(picks.at[pl.ds(0, 15)], picks.at[pl.ds(0, 15)], line_send).wait()
    to_mate.wait_send()
    for part in range(3):
        ref = panel.at[part]
        pltpu.make_async_copy(ref, ref, plane_send).wait()
    ref = panel.at[3, pl.ds(0, 3)]
    pltpu.make_async_copy(ref, ref, plane_send).wait()
    to_out.wait_send()
    pltpu.make_async_copy(outbox, outbox, out_recv).wait()


def on_device(records, usable, panel_ids):
    tables = [jnp.asarray(t) for t in make_tables()]
    vmem = pl.BlockSpec(memory_space=pltpu.VMEM)
    dma = pltpu.SemaphoreType.DMA
    return pl.pallas_call(
        kernel,
        out_shape=jax.ShapeDtypeStruct((2, 64, 4, NLAG), BF16),
        in_specs=[pl.BlockSpec(memory_space=pltpu.SMEM)] + [pl.BlockSpec(memory_space=pltpu.HBM)] * 5,
        out_specs=vmem,
        scratch_shapes=[
            pltpu.VMEM((4, 4, 2048), BF16),
            pltpu.VMEM((4, 2048), jnp.int32),
            pltpu.VMEM((1664, 256), BF16),
            pltpu.VMEM((2, 16, 128), F32),
            pltpu.VMEM((16, 16, 128), BF16),
            pltpu.VMEM((16, 16, 128), BF16),
            pltpu.VMEM((4, 4, 2, 8, 16, 128), BF16),
            pltpu.VMEM((16, 16, 128), BF16),
            pltpu.VMEM((16, 16, 128), BF16),
            pltpu.VMEM((2, 16, 4, 8, 128), F32),
            pltpu.VMEM((512, 2048), BF16),
            pltpu.VMEM((2048, NLAG), BF16),
            pltpu.VMEM((512, 128), F32),
            pltpu.VMEM((64, 4, NLAG), BF16),
            dma((5,)),
            dma,
            dma,
            dma,
            dma,
            dma,
            dma,
            dma,
            dma((2, 4, 4)),
            dma,
            dma,
        ],
        compiler_params=pltpu.CompilerParams(
            collective_id=0, has_side_effects=True, vmem_limit_bytes=60 * 1024 * 1024
        ),
    )(panel_ids, records, usable.T, *tables)


def solution(mesh):
    return jax.shard_map(
        on_device,
        mesh=mesh,
        in_specs=(P(("grp", "dev"), None, None), P(), P()),
        out_specs=P(None, None, ("grp", "dev"), None),
        check_vma=False,
    )
```

```python
import math

import jax
import jax.numpy as jnp
import ml_dtypes
import numpy as np
from jax import lax
from jax.experimental import pallas as pl
from jax.experimental.pallas import tpu as pltpu
from jax.sharding import PartitionSpec as P

L = 2048
NF = 1024
RADIUS = 64
NLAG = 512
F32 = jnp.float32
BF16 = jnp.bfloat16
MESH = pl.DeviceIdType.MESH


def bins_of():
    lane = np.arange(128)
    bins = np.zeros((8, 128), np.int64)
    bins[0] = np.where(lane < 64, 16 * lane + 8, 16 * (lane - 63))
    for r in range(1, 8):
        bins[r] = 16 * lane + r
    return bins


def split_table(table):
    high = table.astype(ml_dtypes.bfloat16)
    low = (table - high.astype(np.float64)).astype(ml_dtypes.bfloat16)
    return high, low


def make_tables():
    bins = bins_of()
    natural = np.where(bins > NF, L - bins, bins)
    b = np.arange(128)
    angle = 2 * np.pi * np.outer(b, b) / 128
    cos, sin = np.cos(angle), np.sin(angle)
    dft = np.block([[cos, -sin], [sin, cos]])
    special = np.zeros((384, 256))
    for lane in range(64):
        special[128:256, lane] = cos[:, lane]
        special[256:384, lane] = sin[:, lane]
        special[128:256, 128 + lane] = -sin[:, lane]
        special[256:384, 128 + lane] = cos[:, lane]
    for lane in range(64, 128):
        special[0:128, lane] = np.cos(2 * np.pi * b * (lane - 63) / 128)
        special[0:128, 128 + lane] = -np.sin(2 * np.pi * b * (lane - 63) / 128)
    r = np.arange(16)[:, None]
    twiddle = 2 * np.pi * r * b[None, :] / L
    turn = np.concatenate([np.cos(twiddle), np.sin(twiddle)])

    def near(left, right):
        return (np.abs(natural[left][:, None] - natural[right][None, :]) <= RADIUS).astype(np.float64)

    band = np.concatenate([near(1, 2), near(2, 2), near(3, 2), near(0, 2)], axis=0)
    band0 = np.concatenate([near(1, 0), near(0, 0)], axis=0)
    lag = np.arange(NLAG) - NLAG // 2
    phase = 2 * np.pi * ((bins.reshape(-1)[:, None] * lag[None, :]) % L) / L
    ltable = np.concatenate([np.cos(phase), -np.sin(phase)], axis=0) / math.sqrt(NF)
    bf = ml_dtypes.bfloat16
    turns = np.zeros((128, 256), bf)
    turns[:32, :128], turns[:32, 128:] = split_table(turn)
    rows = [
        ltable.astype(bf),
        np.concatenate(split_table(special), axis=1),
        np.concatenate(split_table(dft), axis=1),
        np.concatenate([band[128 * n : 128 * n + 128] for n in range(4)], axis=1).astype(bf),
        np.concatenate([band0[:128].astype(bf), band0[128:].astype(bf), turns], axis=1),
    ]
    return np.concatenate(rows, axis=0)


def split(values):
    high = values.astype(BF16)
    return high, (values - high.astype(F32)).astype(BF16)


def dot(left, right):
    return jnp.dot(left, right, preferred_element_type=F32)


def transform(rows, tab_ref):
    count = rows.shape[0]
    x = [rows[:, 128 * a : 128 * a + 128] for a in range(16)]
    even = [None] + [x[a] + x[16 - a] for a in range(1, 8)]
    odd = [None] + [x[a] - x[16 - a] for a in range(1, 8)]
    parts_re, parts_im = [], []
    for r in range(9):
        re = x[0] + x[8] if r % 2 == 0 else x[0] - x[8]
        im = None
        for a in range(1, 8):
            c = math.cos(2 * math.pi * ((a * r) % 16) / 16)
            s = math.sin(2 * math.pi * ((a * r) % 16) / 16)
            if abs(c) > 1e-9:
                re = re + even[a] * c
            if abs(s) > 1e-9:
                im = odd[a] * -s if im is None else im + odd[a] * -s
        parts_re.append(re)
        parts_im.append(im)
    turn = tab_ref[768:800, 256:384].astype(F32) + tab_ref[768:800, 384:512].astype(F32)
    turned = []
    for r in range(1, 8):
        c, s = turn[r : r + 1], turn[16 + r : 17 + r]
        turned.append(jnp.concatenate([parts_re[r] * c + parts_im[r] * s, parts_im[r] * c - parts_re[r] * s], axis=1))
    y = jnp.concatenate(turned, axis=0)
    c, s = turn[8:9], turn[24:25]
    y0 = jnp.concatenate([parts_re[0], parts_re[8] * c, -(parts_re[8] * s)], axis=1)

    def product(values, at):
        high, low = split(values)
        n, depth = values.shape
        both = dot(jnp.concatenate([high, low], axis=0), tab_ref[at : at + depth, :256])
        return both[:n] + both[n:] + dot(high, tab_ref[at : at + depth, 256:])

    spectra = product(y, 384)
    spectra0 = product(y0, 0)
    re = [spectra0[:, :128]] + [spectra[count * j : count * j + count, :128] for j in range(7)]
    im = [spectra0[:, 128:]] + [spectra[count * j : count * j + count, 128:] for j in range(7)]
    return re, im


def running_mean(amplitude, tab_ref):
    count = amplitude[0].shape[0]
    below = [None, jnp.zeros_like(amplitude[0])]
    for r in range(2, 9):
        below.append(below[r - 1] + amplitude[r - 1])
    total = below[8]
    left = jnp.concatenate(
        [
            jnp.concatenate([below[r], amplitude[r], total - below[r] - amplitude[r], amplitude[0]], axis=1)
            for r in range(1, 8)
        ],
        axis=0,
    )
    left0 = jnp.concatenate([total, amplitude[0]], axis=1)

    def product(values, at):
        both = jnp.concatenate(split(values), axis=0)
        n = values.shape[0]
        sums = dot(both[:, :128], tab_ref[at : at + 128, :128])
        for k in range(1, values.shape[1] // 128):
            piece = slice(128 * k, 128 * k + 128)
            sums = sums + dot(both[:, piece], tab_ref[at : at + 128, piece])
        return sums[:n] + sums[n:]

    sums = product(left, 640)
    sums0 = product(left0, 768)
    scale = 1.0 / (2 * RADIUS + 1)
    return [sums0 * scale] + [sums[count * j : count * j + count] * scale for j in range(7)]


def kernel(
    panel_ids_ref,
    x_hbm,
    usable_hbm,
    tables_hbm,
    out_ref,
    x_ref,
    usable_ref,
    tab_ref,
    units,
    picks,
    panel,
    own,
    other,
    recv,
    lhs,
    lt_ref,
    scales,
    outbox,
    in_sem,
    unit_send,
    unit_recv,
    other_send,
    other_recv,
    line_send,
    line_recv,
    plane_send,
    plane_recv,
    out_send,
    out_recv,
):
    g = lax.axis_index("grp")
    d = lax.axis_index("dev")
    z_lo, c = g // 2, g % 2
    z_hi, xx, yy = d // 16, (d // 4) % 4, d % 4
    mate = z_lo * 2 + (1 - c)

    loads = [
        pltpu.make_async_copy(source, target, in_sem.at[n])
        for n, (source, target) in enumerate(
            [
                (x_hbm, x_ref),
                (tables_hbm.at[pl.ds(2048, 896)], tab_ref),
                (usable_hbm, usable_ref),
                (tables_hbm.at[pl.ds(0, 2048)], lt_ref),
            ]
        )
    ]
    for load in loads:
        load.start()

    barrier = pltpu.get_barrier_semaphore()

    def hello(grp, dev):
        pl.semaphore_signal(barrier, inc=1, device_id=(grp, dev), device_id_type=MESH)

    held = 1 - (z_lo // 4 - z_hi) * (z_lo // 4 - z_hi)
    quad = z_lo % 4
    is_holder = held == 1

    def holder_chip(side, n):
        return side * (7 - n) + (1 - side) * n

    def hello_holder(n, carry):
        side = n // 4
        grp, dev = holder_chip(side, n % 4) * 2 + c, side * 16 + d % 16

        @pl.when((grp - g) * (grp - g) + (dev - d) * (dev - d) > 0)
        def _():
            hello(grp, dev)

        return carry

    lax.fori_loop(0, 8, hello_holder, 0)

    def hello_grp(n, carry):
        hello((g + n) % 16, d)
        return carry

    @pl.when(is_holder)
    def _():
        lax.fori_loop(1, 16, hello_grp, 0)

    @pl.when(jnp.logical_not(is_holder))
    def _():
        hello(mate, d)

    def hello_plane(k, carry):
        hello(g, z_hi * 16 + ((xx + k) % 4) * 4 + yy)
        hello(g, z_hi * 16 + xx * 4 + (yy + k) % 4)
        return carry

    lax.fori_loop(1, 4, hello_plane, 0)

    for load in loads[:3]:
        load.wait()
    rows = jnp.concatenate([x_ref[ch].astype(F32) for ch in range(4)], axis=0)
    spec_re, spec_im = transform(rows, tab_ref)
    amplitude = [jnp.sqrt(re * re + im * im) for re, im in zip(spec_re, spec_im)]
    smooth = running_mean(amplitude, tab_ref)

    lane16 = lax.broadcasted_iota(jnp.int32, (16, 128), 1)
    row16 = lax.broadcasted_iota(jnp.int32, (16, 128), 0)

    def mask_of(group):
        block = usable_ref[:, pl.ds(pl.multiple_of(group * 128, 128), 128)].astype(F32)
        tiled = jnp.concatenate([block] * 4, axis=0)
        chosen = jnp.where(lane16 == 4 * d + row16 // 4, tiled, 0.0)
        return jnp.sum(chosen, axis=1, keepdims=True)

    own_mask = mask_of(g)
    mate_mask = mask_of(mate)

    upper = [(jnp.full((8, 128), panel_ids_ref[t]) & 1) == 1 for t in range(2)]
    for k in range(8):
        inverse = 1.0 / (smooth[k] + 1e-06)
        re = (spec_re[k] * inverse).astype(BF16).astype(F32) * own_mask
        im = (spec_im[k] * inverse).astype(BF16).astype(F32) * own_mask
        own[k] = re.astype(BF16)
        own[8 + k] = im.astype(BF16)
        for t in range(2):
            pair = jnp.concatenate(
                [jnp.where(upper[t], re[8:], re[:8]), jnp.where(upper[t], im[8:], im[:8])], axis=0
            )
            units[(k // 2) * 2 + t, k % 2] = pair.astype(BF16)

    pl.semaphore_wait(barrier, 15 + 13 * held)

    def send_unit(n, carry):
        chip = holder_chip(z_hi, n // 2)
        to = chip * 2 + n % 2

        @pl.when(to != g)
        def _():
            pltpu.make_async_remote_copy(
                src_ref=units.at[(chip % 4) * 2 + n % 2],
                dst_ref=picks.at[g],
                send_sem=unit_send,
                recv_sem=unit_recv,
                device_id=(to, d),
                device_id_type=MESH,
            ).start()

        return carry

    lax.fori_loop(0, 8, send_unit, 0)
    to_mate = pltpu.make_async_remote_copy(
        src_ref=own,
        dst_ref=other,
        send_sem=other_send,
        recv_sem=other_recv,
        device_id=(mate, d),
        device_id_type=MESH,
    )
    to_mate.start()
    chosen = panel_ids_ref[c]
    owner = jnp.full((16, 128), chosen) >> 1

    def wait_for(ref, sem):
        pltpu.make_async_copy(ref, ref, sem).wait()

    mine = panel.at[xx, yy, z_hi, pl.ds(2 * quad, 2)]

    def send_line(n, carry):
        z = (n // 2) * (1 - n % 2) + (15 - n // 2) * (n % 2)
        grp, dev = (z % 8) * 2 + c, (z // 8) * 16 + d % 16

        @pl.when((grp - g) * (grp - g) + (dev - d) * (dev - d) > 0)
        def _():
            pltpu.make_async_remote_copy(
                src_ref=mine,
                dst_ref=mine,
                send_sem=line_send,
                recv_sem=line_recv.at[z_hi],
                device_id=(grp, dev),
                device_id_type=MESH,
            ).start()

        return carry

    @pl.when(is_holder)
    def _():
        picks[g] = units[quad * 2 + c]
        wait_for(picks.at[pl.ds(0, 15)], unit_recv)
        for b in range(2):
            pick = jnp.where(owner == 0, picks[0, b].astype(F32), 0.0)
            for k in range(1, 16):
                pick = jnp.where(owner == k, picks[k, b].astype(F32), pick)
            panel[xx, yy, z_hi, 2 * quad + b] = pick.astype(BF16)
        lax.fori_loop(0, 16, send_line, 0)

    low = lax.broadcasted_iota(jnp.int32, (8, 128), 0) < 4

    def spread(side, source):
        def one(p, carry):
            tile = source[p].astype(F32)
            for pair in range(2):
                rows8 = tile[8 * pair : 8 * pair + 8]
                turned = pltpu.roll(rows8, 4, 0)
                recv[side, p, 2 * pair] = jnp.where(low, rows8, turned)
                recv[side, p, 2 * pair + 1] = jnp.where(low, turned, rows8)
            return carry

        lax.fori_loop(0, 16, one, 0)

    spread(0, own)
    to_mate.wait_recv()
    spread(1, other)

    block = usable_ref[:, :128]
    for k in range(1, 16):
        block = jnp.where(owner[:4] == k, usable_ref[:, 128 * k : 128 * k + 128], block)
    block = block.astype(F32)
    weights = jnp.concatenate([block] * 8, axis=0) * jnp.concatenate([own_mask, mate_mask], axis=0)
    row = lax.broadcasted_iota(jnp.int32, (512, 128), 0)
    lane = lax.broadcasted_iota(jnp.int32, (512, 128), 1)
    at_x = (xx + row // 128) % 4
    at_y = (yy + (row // 32) % 4) % 4
    at_dev = ((row // 16) % 2) * 16 + at_x * 4 + at_y
    half = jnp.full((512, 128), chosen) & 1
    picked = jnp.where(lane == at_dev * 4 + half * 2 + (row // 4) % 2, 1.0, 0.0).astype(BF16)
    counts = lax.dot_general(picked, weights.astype(BF16), (((1,), (1,)), ((), ())), preferred_element_type=F32)
    row32 = lax.broadcasted_iota(jnp.int32, (512, 32), 0)
    lane32 = lax.broadcasted_iota(jnp.int32, (512, 32), 1)
    match = lane32 // 4 == ((row32 // 8) % 2) * 4 + row32 % 4
    count = jnp.sum(jnp.where(match, counts, 0.0), axis=1, keepdims=True)
    scales[...] = jnp.broadcast_to(1.0 / jnp.maximum(count, 1.0), (512, 128))

    def send_block(h, bx, by, tx, ty):
        pltpu.make_async_remote_copy(
            src_ref=panel.at[bx, by, h],
            dst_ref=panel.at[bx, by, h],
            send_sem=plane_send,
            recv_sem=plane_recv.at[h, bx, by],
            device_id=(g, z_hi * 16 + tx * 4 + ty),
            device_id_type=MESH,
        ).start()

    def wait_block(h, bx, by):
        wait_for(panel.at[bx, by, h], plane_recv.at[h, bx, by])

    def to_x(h):
        def send(k, carry):
            send_block(h, xx, yy, (xx + k) % 4, yy)
            return carry

        lax.fori_loop(1, 4, send, 0)

    def to_y(h):
        def send(k, carry):
            send_block(h, xx, yy, xx, (yy + k) % 4)
            return carry

        lax.fori_loop(1, 4, send, 0)

    def wait_line(h):
        missing = held * (1 - (z_hi - h) * (z_hi - h))

        @pl.when(missing == 1)
        def _():
            wait_for(panel.at[0, 0, 0, pl.ds(0, 6)], line_recv.at[h])

        @pl.when(missing == 0)
        def _():
            wait_for(panel.at[0, 0, 0], line_recv.at[h])

    wait_line(0)
    to_x(0)
    to_y(0)
    wait_line(1)
    to_y(1)
    to_x(1)

    def forward(k, carry):
        bx, by = (xx + k) % 4, (yy + k) % 4
        wait_block(0, bx, yy)

        def on_y(m, inner):
            send_block(0, bx, yy, xx, (yy + m) % 4)
            return inner

        lax.fori_loop(1, 4, on_y, 0)
        wait_block(1, xx, by)

        def on_x(m, inner):
            send_block(1, xx, by, (xx + m) % 4, yy)
            return inner

        lax.fori_loop(1, 4, on_x, 0)
        return carry

    lax.fori_loop(1, 4, forward, 0)

    wait_block(1, (xx + 1) % 4, yy)
    wait_block(1, (xx + 2) % 4, yy)
    wait_block(1, (xx + 3) % 4, yy)
    wait_block(0, xx, (yy + 1) % 4)
    wait_block(0, xx, (yy + 2) % 4)
    wait_block(0, xx, (yy + 3) % 4)
    loads[3].wait()

    sub = lax.broadcasted_iota(jnp.int32, (8, 128), 0)
    even1 = sub % 2 == 0
    even2 = (sub // 2) % 2 == 0

    def fold(v):
        first = jnp.where(even1, v[0] + pltpu.roll(v[0], 7, 0), v[1] + pltpu.roll(v[1], 1, 0))
        second = jnp.where(even1, v[2] + pltpu.roll(v[2], 7, 0), v[3] + pltpu.roll(v[3], 1, 0))
        return jnp.where(even2, first + pltpu.roll(first, 6, 0), second + pltpu.roll(second, 2, 0))

    def cross(line, bx, by, h):
        slot = line * 2 + h
        for k in range(8):
            both = panel[bx, by, h, k].astype(F32)
            a, b = both[:8], both[8:]
            re_rows, im_rows = [], []
            for side in range(2):
                re, im = [], []
                for r in range(4):
                    cc, ee = recv[side, k, r], recv[side, 8 + k, r]
                    re.append(a * cc + b * ee)
                    im.append(b * cc - a * ee)
                re_rows.append(fold(re))
                im_rows.append(fold(im))
            at = pl.ds(pl.multiple_of(slot * 16, 16), 16)
            lhs[at, 128 * k : 128 * k + 128] = jnp.concatenate(re_rows, axis=0).astype(BF16)
            lhs[at, 1024 + 128 * k : 1152 + 128 * k] = jnp.concatenate(im_rows, axis=0).astype(BF16)

    def quarter(q, carry):
        bx = (xx + q) % 4

        def one_line(m, inner):
            by = (yy + m) % 4
            cross(q * 4 + m, bx, by, 0)
            cross(q * 4 + m, bx, by, 1)
            return inner

        lax.fori_loop(0, 4, one_line, 0)
        at = pl.ds(pl.multiple_of(q * 128, 128), 128)
        lagged = dot(lhs[at, :], lt_ref[...]) * jnp.concatenate([scales[at, :]] * 4, axis=1)
        for m in range(4):
            by = (yy + m) % 4
            for h in range(2):
                base = m * 32 + h * 16
                s = (h * 16 + bx * 4 + by) * 2
                for i in range(2):
                    out_ref[c, s + i] = lagged[base + 4 * i : base + 4 * i + 4].astype(BF16)
                    outbox[s + i] = lagged[base + 8 + 4 * i : base + 12 + 4 * i].astype(BF16)
        for h in range(2):
            eight = pl.ds(h * 32 + bx * 8, 8)
            pltpu.make_async_remote_copy(
                src_ref=outbox.at[eight],
                dst_ref=out_ref.at[c, eight],
                send_sem=out_send,
                recv_sem=out_recv,
                device_id=(mate, d),
                device_id_type=MESH,
            ).start()
        return carry

    quarter(0, 0)

    def later(q, carry):
        bx = (xx + q) % 4

        def wait_line(m, inner):
            by = (yy + m) % 4
            wait_block(0, bx, by)
            wait_block(1, bx, by)
            return inner

        lax.fori_loop(1, 4, wait_line, 0)
        return quarter(q, carry)

    lax.fori_loop(1, 4, later, 0)

    @pl.when(is_holder)
    def _():
        wait_for(picks.at[pl.ds(0, 7)], unit_send)
        wait_for(picks.at[pl.ds(0, 15)], line_send)

    @pl.when(jnp.logical_not(is_holder))
    def _():
        wait_for(picks.at[pl.ds(0, 8)], unit_send)

    to_mate.wait_send()
    for part in range(3):
        wait_for(panel.at[part], plane_send)
    wait_for(panel.at[3, pl.ds(0, 3)], plane_send)
    wait_for(outbox, out_send)
    wait_for(outbox, out_recv)


def on_device(records, usable, panel_ids):
    vmem = pl.BlockSpec(memory_space=pltpu.VMEM)
    dma = pltpu.SemaphoreType.DMA
    return pl.pallas_call(
        kernel,
        out_shape=jax.ShapeDtypeStruct((2, 64, 4, NLAG), BF16),
        in_specs=[pl.BlockSpec(memory_space=pltpu.SMEM)] + [pl.BlockSpec(memory_space=pltpu.HBM)] * 3,
        out_specs=vmem,
        scratch_shapes=[
            pltpu.VMEM((4, 4, 2048), BF16),
            pltpu.VMEM((4, 2048), jnp.int32),
            pltpu.VMEM((896, 512), BF16),
            pltpu.VMEM((8, 2, 16, 128), BF16),
            pltpu.VMEM((16, 2, 16, 128), BF16),
            pltpu.VMEM((4, 4, 2, 8, 16, 128), BF16),
            pltpu.VMEM((16, 16, 128), BF16),
            pltpu.VMEM((16, 16, 128), BF16),
            pltpu.VMEM((2, 16, 4, 8, 128), F32),
            pltpu.VMEM((512, 2048), BF16),
            pltpu.VMEM((2048, NLAG), BF16),
            pltpu.VMEM((512, 128), F32),
            pltpu.VMEM((64, 4, NLAG), BF16),
            dma((4,)),
            dma,
            dma,
            dma,
            dma,
            dma,
            dma((2,)),
            dma,
            dma((2, 4, 4)),
            dma,
            dma,
        ],
        compiler_params=pltpu.CompilerParams(
            collective_id=0, has_side_effects=True, vmem_limit_bytes=52 * 1024 * 1024
        ),
    )(*[pltpu.with_memory_space_constraint(a, pltpu.HBM) for a in (panel_ids, records, usable.T, jnp.asarray(make_tables()))])


def solution(mesh):
    return jax.shard_map(
        on_device,
        mesh=mesh,
        in_specs=(P(("grp", "dev"), None, None), P(), P()),
        out_specs=P(None, None, ("grp", "dev"), None),
        check_vma=False,
    )
```

```python
import math

import jax
import jax.numpy as jnp
import ml_dtypes
import numpy as np
from jax import lax
from jax.experimental import pallas as pl
from jax.experimental.pallas import tpu as pltpu
from jax.sharding import PartitionSpec as P

L = 2048
NF = 1024
RADIUS = 64
NLAG = 512
FIRST = 12
SECOND = 22
F32 = jnp.float32
BF16 = jnp.bfloat16
MESH = pl.DeviceIdType.MESH


def bins_of():
    lane = np.arange(128)
    bins = np.zeros((8, 128), np.int64)
    bins[0] = np.where(lane < 64, 16 * lane + 8, 16 * (lane - 63))
    for r in range(1, 8):
        bins[r] = 16 * lane + r
    return bins


def split_table(table):
    high = table.astype(ml_dtypes.bfloat16)
    low = (table - high.astype(np.float64)).astype(ml_dtypes.bfloat16)
    return high, low


def make_tables():
    bins = bins_of()
    natural = np.where(bins > NF, L - bins, bins)
    b = np.arange(128)
    angle = 2 * np.pi * np.outer(b, b) / 128
    cos, sin = np.cos(angle), np.sin(angle)
    dft = np.block([[cos, -sin], [sin, cos]])
    special = np.zeros((384, 256))
    for lane in range(64):
        special[128:256, lane] = cos[:, lane]
        special[256:384, lane] = sin[:, lane]
        special[128:256, 128 + lane] = -sin[:, lane]
        special[256:384, 128 + lane] = cos[:, lane]
    for lane in range(64, 128):
        special[0:128, lane] = np.cos(2 * np.pi * b * (lane - 63) / 128)
        special[0:128, 128 + lane] = -np.sin(2 * np.pi * b * (lane - 63) / 128)
    r = np.arange(16)[:, None]
    twiddle = 2 * np.pi * r * b[None, :] / L
    turn = np.concatenate([np.cos(twiddle), np.sin(twiddle)])

    def near(left, right):
        return (np.abs(natural[left][:, None] - natural[right][None, :]) <= RADIUS).astype(np.float64)

    band = np.concatenate([near(1, 2), near(2, 2), near(3, 2), near(0, 2)], axis=0)
    band0 = np.concatenate([near(1, 0), near(0, 0)], axis=0)
    lag = np.arange(NLAG) - NLAG // 2
    phase = 2 * np.pi * ((bins.reshape(-1)[:, None] * lag[None, :]) % L) / L
    ltable = np.concatenate([np.cos(phase), -np.sin(phase)], axis=0) / math.sqrt(NF)
    bf = ml_dtypes.bfloat16
    turns = np.zeros((128, 256), bf)
    turns[:32, :128], turns[:32, 128:] = split_table(turn)
    rows = [
        ltable.astype(bf),
        np.concatenate(split_table(special), axis=1),
        np.concatenate(split_table(dft), axis=1),
        np.concatenate([band[128 * n : 128 * n + 128] for n in range(4)], axis=1).astype(bf),
        np.concatenate([band0[:128].astype(bf), band0[128:].astype(bf), turns], axis=1),
    ]
    return np.concatenate(rows, axis=0)


def split(values):
    high = values.astype(BF16)
    return high, (values - high.astype(F32)).astype(BF16)


def dot(left, right):
    return jnp.dot(left, right, preferred_element_type=F32)


def transform(rows, tab_ref):
    count = rows.shape[0]
    x = [rows[:, 128 * a : 128 * a + 128] for a in range(16)]
    even = [None] + [x[a] + x[16 - a] for a in range(1, 8)]
    odd = [None] + [x[a] - x[16 - a] for a in range(1, 8)]
    parts_re, parts_im = [], []
    for r in range(9):
        re = x[0] + x[8] if r % 2 == 0 else x[0] - x[8]
        im = None
        for a in range(1, 8):
            c = math.cos(2 * math.pi * ((a * r) % 16) / 16)
            s = math.sin(2 * math.pi * ((a * r) % 16) / 16)
            if abs(c) > 1e-9:
                re = re + even[a] * c
            if abs(s) > 1e-9:
                im = odd[a] * -s if im is None else im + odd[a] * -s
        parts_re.append(re)
        parts_im.append(im)
    turn = tab_ref[768:800, 256:384].astype(F32) + tab_ref[768:800, 384:512].astype(F32)
    turned = []
    for r in range(1, 8):
        c, s = turn[r : r + 1], turn[16 + r : 17 + r]
        turned.append(jnp.concatenate([parts_re[r] * c + parts_im[r] * s, parts_im[r] * c - parts_re[r] * s], axis=1))
    y = jnp.concatenate(turned, axis=0)
    c, s = turn[8:9], turn[24:25]
    y0 = jnp.concatenate([parts_re[0], parts_re[8] * c, -(parts_re[8] * s)], axis=1)

    def product(values, at):
        high, low = split(values)
        n, depth = values.shape
        both = dot(jnp.concatenate([high, low], axis=0), tab_ref[at : at + depth, :256])
        return both[:n] + both[n:] + dot(high, tab_ref[at : at + depth, 256:])

    spectra = product(y, 384)
    spectra0 = product(y0, 0)
    re = [spectra0[:, :128]] + [spectra[count * j : count * j + count, :128] for j in range(7)]
    im = [spectra0[:, 128:]] + [spectra[count * j : count * j + count, 128:] for j in range(7)]
    return re, im


def running_mean(amplitude, tab_ref):
    count = amplitude[0].shape[0]
    below = [None, jnp.zeros_like(amplitude[0])]
    for r in range(2, 9):
        below.append(below[r - 1] + amplitude[r - 1])
    total = below[8]
    left = jnp.concatenate(
        [
            jnp.concatenate([below[r], amplitude[r], total - below[r] - amplitude[r], amplitude[0]], axis=1)
            for r in range(1, 8)
        ],
        axis=0,
    )
    left0 = jnp.concatenate([total, amplitude[0]], axis=1)

    def product(values, at):
        both = jnp.concatenate(split(values), axis=0)
        n = values.shape[0]
        sums = dot(both[:, :128], tab_ref[at : at + 128, :128])
        for k in range(1, values.shape[1] // 128):
            piece = slice(128 * k, 128 * k + 128)
            sums = sums + dot(both[:, piece], tab_ref[at : at + 128, piece])
        return sums[:n] + sums[n:]

    sums = product(left, 640)
    sums0 = product(left0, 768)
    scale = 1.0 / (2 * RADIUS + 1)
    return [sums0 * scale] + [sums[count * j : count * j + count] * scale for j in range(7)]


def kernel(
    panel_ids_ref,
    x_hbm,
    usable_hbm,
    tables_hbm,
    out_ref,
    x_ref,
    usable_ref,
    tab_ref,
    units,
    picks,
    panel,
    own,
    other,
    recv,
    lhs,
    lagged,
    lt_ref,
    scales,
    outbox,
    in_sem,
    unit_send,
    unit_recv,
    other_send,
    other_recv,
    line_send,
    line_recv,
    relay_send,
    plane_send,
    plane_recv,
    out_send,
    out_recv,
):
    g = lax.axis_index("grp")
    d = lax.axis_index("dev")
    z_lo, c = g // 2, g % 2
    z_hi, xx, yy = d // 16, (d // 4) % 4, d % 4
    mate = z_lo * 2 + (1 - c)

    loads = [
        pltpu.make_async_copy(source, target, in_sem.at[n])
        for n, (source, target) in enumerate(
            [
                (x_hbm, x_ref),
                (tables_hbm.at[pl.ds(2048, 896)], tab_ref),
                (usable_hbm, usable_ref),
                (tables_hbm.at[pl.ds(0, 2048)], lt_ref),
            ]
        )
    ]
    for load in loads:
        load.start()

    barrier = pltpu.get_barrier_semaphore()

    def hello(grp, dev):
        pl.semaphore_signal(barrier, inc=1, device_id=(grp, dev), device_id_type=MESH)

    held = 1 - (z_lo // 4 - z_hi) * (z_lo // 4 - z_hi)
    quad = z_lo % 4
    is_holder = held == 1

    def holder_chip(side, n):
        return side * (7 - n) + (1 - side) * n

    zz = z_hi * 8 + z_lo
    is_far = z_hi * (1 - z_lo // 4) == 1
    is_relay = (zz - 7) * (zz - 12) == 0

    def line_device(z):
        return (z % 8) * 2 + c, (z // 8) * 16 + d % 16

    def hello_holder(n, carry):
        side = n // 4
        z = side * 8 + holder_chip(side, n % 4)

        @pl.when(z != zz)
        def _():
            hello(*line_device(z))

        return carry

    @pl.when(jnp.logical_not(is_far))
    def _():
        lax.fori_loop(0, 8, hello_holder, 0)

    @pl.when(is_far)
    def _():
        hello(*line_device(7 + 5 * ((zz - 8) // 2)))

    def hello_grp(n, carry):
        hello((g + n) % 16, d)
        return carry

    @pl.when(is_holder)
    def _():
        lax.fori_loop(1, 16, hello_grp, 0)

    @pl.when(jnp.logical_not(is_holder))
    def _():
        hello(mate, d)

    def hello_plane(n, carry):
        i, j = 2 - n // 4 + 3 * (n // 8) - 2 * (n // 12), 2 - n % 4 + 3 * ((n % 4) // 2) - 2 * ((n % 4) // 3)
        hello(g, z_hi * 16 + ((xx + i) % 4) * 4 + (yy + j) % 4)
        return carry

    lax.fori_loop(0, 15, hello_plane, 0)

    for load in loads[:3]:
        load.wait()
    loaded = [x_ref[ch].astype(F32) for ch in range(4)]
    rows = jnp.concatenate(
        [loaded[2 * pair + i][w : w + 1] for pair in range(2) for w in range(4) for i in range(2)], axis=0
    )
    spec_re, spec_im = transform(rows, tab_ref)
    amplitude = [jnp.sqrt(re * re + im * im) for re, im in zip(spec_re, spec_im)]
    smooth = running_mean(amplitude, tab_ref)

    lane16 = lax.broadcasted_iota(jnp.int32, (16, 128), 1)
    row16 = lax.broadcasted_iota(jnp.int32, (16, 128), 0)

    def twice(block):
        return jnp.concatenate([block[w // 2 : w // 2 + 1] for w in range(8)], axis=0)

    def mask_of(group):
        block = usable_ref[:, pl.ds(pl.multiple_of(group * 128, 128), 128)].astype(F32)
        tiled = jnp.concatenate([twice(block)] * 2, axis=0)
        chosen = jnp.where(lane16 == 4 * d + (row16 // 8) * 2 + row16 % 2, tiled, 0.0)
        return jnp.sum(chosen, axis=1, keepdims=True)

    own_mask = mask_of(g)
    mate_mask = mask_of(mate)

    upper = [(jnp.full((8, 128), panel_ids_ref[t]) & 1) == 1 for t in range(2)]
    for k in range(8):
        inverse = 1.0 / (smooth[k] + 1e-06)
        re = (spec_re[k] * inverse).astype(BF16).astype(F32) * own_mask
        im = (spec_im[k] * inverse).astype(BF16).astype(F32) * own_mask
        own[k] = re.astype(BF16)
        own[8 + k] = im.astype(BF16)
        for t in range(2):
            pair = jnp.concatenate(
                [jnp.where(upper[t], re[8:], re[:8]), jnp.where(upper[t], im[8:], im[:8])], axis=0
            )
            units[(k // 2) * 2 + t, k % 2] = pair.astype(BF16)

    @pl.when(is_relay)
    def _():
        pl.semaphore_wait(barrier, 26 + 9 * held)

    @pl.when(jnp.logical_not(is_relay))
    def _():
        pl.semaphore_wait(barrier, 24 + 9 * held)


    def send_unit(n, carry):
        chip = holder_chip(z_hi, n // 2)
        to = chip * 2 + n % 2

        @pl.when(to != g)
        def _():
            pltpu.make_async_remote_copy(
                src_ref=units.at[(chip % 4) * 2 + n % 2],
                dst_ref=picks.at[g],
                send_sem=unit_send,
                recv_sem=unit_recv,
                device_id=(to, d),
                device_id_type=MESH,
            ).start()

        return carry

    lax.fori_loop(0, 8, send_unit, 0)
    to_mate = pltpu.make_async_remote_copy(
        src_ref=own,
        dst_ref=other,
        send_sem=other_send,
        recv_sem=other_recv,
        device_id=(mate, d),
        device_id_type=MESH,
    )
    to_mate.start()
    chosen = panel_ids_ref[c]
    owner = jnp.full((16, 128), chosen) >> 1

    sub = lax.broadcasted_iota(jnp.int32, (8, 128), 0)
    first_of_pair = sub % 2 == 0

    def spread(side, source):
        def one(p, carry):
            tile = source[p].astype(F32)
            for pair in range(2):
                rows8 = tile[8 * pair : 8 * pair + 8]
                recv[side, p, 2 * pair] = jnp.where(first_of_pair, rows8, pltpu.roll(rows8, 1, 0))
                recv[side, p, 2 * pair + 1] = jnp.where(first_of_pair, pltpu.roll(rows8, 7, 0), rows8)
            return carry

        lax.fori_loop(0, 16, one, 0)

    spread(0, own)
    to_mate.wait_recv()
    spread(1, other)

    block = usable_ref[:, :128]
    for k in range(1, 16):
        block = jnp.where(owner[:4] == k, usable_ref[:, 128 * k : 128 * k + 128], block)
    block = block.astype(F32)
    weights = jnp.concatenate([twice(block)] * 4, axis=0) * jnp.concatenate([own_mask, mate_mask], axis=0)
    row = lax.broadcasted_iota(jnp.int32, (512, 128), 0)
    lane = lax.broadcasted_iota(jnp.int32, (512, 128), 1)
    at_x = (xx + row // 128) % 4
    at_y = (yy + (row // 32) % 4) % 4
    at_dev = ((row // 16) % 2) * 16 + at_x * 4 + at_y
    half = jnp.full((512, 128), chosen) & 1
    picked = jnp.where(lane == at_dev * 4 + half * 2 + row % 2, 1.0, 0.0).astype(BF16)
    counts = lax.dot_general(picked, weights.astype(BF16), (((1,), (1,)), ((), ())), preferred_element_type=F32)
    row32 = lax.broadcasted_iota(jnp.int32, (512, 32), 0)
    lane32 = lax.broadcasted_iota(jnp.int32, (512, 32), 1)
    match = (lane32 // 8) * 2 + lane32 % 2 == ((row32 // 8) % 2) * 4 + (row32 // 2) % 4
    count = jnp.sum(jnp.where(match, counts, 0.0), axis=1, keepdims=True)
    scales[...] = jnp.broadcast_to(1.0 / jnp.maximum(count, 1.0), (512, 128))

    def wait_for(ref, sem):
        pltpu.make_async_copy(ref, ref, sem).wait()

    mine = panel.at[xx, yy, z_hi, pl.ds(2 * quad, 2)]

    def send_line(n, carry):
        z = (n // 2) * (1 - n % 2) + (15 - n // 2) * (n % 2)
        z = z - 4 * ((n // 8) * (n % 2))

        @pl.when(z != zz)
        def _():
            pltpu.make_async_remote_copy(
                src_ref=mine,
                dst_ref=mine,
                send_sem=line_send,
                recv_sem=line_recv.at[z_hi],
                device_id=line_device(z),
                device_id_type=MESH,
            ).start()

        return carry

    @pl.when(is_holder)
    def _():
        picks[g] = units[quad * 2 + c]
        wait_for(picks.at[pl.ds(0, 15)], unit_recv)
        for b in range(2):
            pick = jnp.where(owner == 0, picks[0, b].astype(F32), 0.0)
            for k in range(1, 16):
                pick = jnp.where(owner == k, picks[k, b].astype(F32), pick)
            panel[xx, yy, z_hi, 2 * quad + b] = pick.astype(BF16)
        lax.fori_loop(0, 12, send_line, 0)

    def wait_line(h):
        missing = held * (1 - (z_hi - h) * (z_hi - h))

        @pl.when(missing == 1)
        def _():
            wait_for(panel.at[0, 0, 0, pl.ds(0, 6)], line_recv.at[h])

        @pl.when(missing == 0)
        def _():
            wait_for(panel.at[0, 0, 0], line_recv.at[h])

        def relay(n, carry):
            ref = panel.at[xx, yy, h]
            pltpu.make_async_remote_copy(
                src_ref=ref,
                dst_ref=ref,
                send_sem=relay_send,
                recv_sem=line_recv.at[h],
                device_id=line_device(8 + n + z_hi * (3 - 2 * n)),
                device_id_type=MESH,
            ).start()
            return carry

        @pl.when(is_relay)
        def _():
            lax.fori_loop(0, 2, relay, 0)

    def offset(n):
        return 2 - n + 3 * (n // 2) - 2 * (n // 3)

    def place_of(h, n):
        i, j = offset(n // 4), offset(n % 4)
        return i * (1 - h) + j * h, j * (1 - h) + i * h

    def to_plane(h):
        ref = panel.at[xx, yy, h]

        def start(tx, ty):
            pltpu.make_async_remote_copy(
                src_ref=ref,
                dst_ref=ref,
                send_sem=plane_send,
                recv_sem=plane_recv.at[h, xx, yy],
                device_id=(g, z_hi * 16 + tx * 4 + ty),
                device_id_type=MESH,
            ).start()

        @pl.when(xx + yy > 0)
        def _():
            start(0, 0)

        def send(n, carry):
            dx, dy = place_of(h, n)
            tx, ty = (xx + dx) % 4, (yy + dy) % 4

            @pl.when(tx + ty > 0)
            def _():
                start(tx, ty)

            return carry

        lax.fori_loop(0, 15, send, 0)

    wait_line(0)
    to_plane(0)
    wait_line(1)
    to_plane(1)

    window = sub // 2
    lower = window < 2
    inner_two = (window == 1) | (window == 2)
    even = window % 2 == 0

    def fold(v):
        u = jnp.where(lower, v[0], v[2]) + pltpu.roll(jnp.where(lower, v[2], v[0]), 4, 0)
        t = jnp.where(inner_two, v[1], v[3]) + pltpu.roll(jnp.where(inner_two, v[3], v[1]), 4, 0)
        return jnp.where(even, u, t) + pltpu.roll(jnp.where(even, t, u), 6, 0)

    def cross(slot, h, dx, dy):
        bx, by = (xx + dx) % 4, (yy + dy) % 4
        at = pl.ds(pl.multiple_of(slot * 16, 16), 16)
        for k in range(8):
            both = panel[bx, by, h, k].astype(F32)
            a, b = both[:8], both[8:]
            re_rows, im_rows = [], []
            for side in range(2):
                re, im = [], []
                for r in range(4):
                    cc, ee = recv[side, k, r], recv[side, 8 + k, r]
                    re.append(a * cc + b * ee)
                    im.append(b * cc - a * ee)
                re_rows.append(fold(re))
                im_rows.append(fold(im))
            lhs[at, 128 * k : 128 * k + 128] = jnp.concatenate(re_rows, axis=0).astype(BF16)
            lhs[at, 1024 + 128 * k : 1152 + 128 * k] = jnp.concatenate(im_rows, axis=0).astype(BF16)

    def finish(first, many, place):
        rows = pl.ds(pl.multiple_of(first * 16, 16), many * 16)
        lagged[: many * 16] = dot(lhs[rows, :], lt_ref[...])

        def one(n, carry):
            h, dx, dy = place(n)
            s = (h * 16 + ((xx + dx) % 4) * 4 + (yy + dy) % 4) * 2
            scale = scales[pl.ds(pl.multiple_of((dx * 8 + dy * 2 + h) * 16, 16), 16), :]
            slot_rows = pl.ds(pl.multiple_of(n * 16, 16), 16)
            values = lagged[slot_rows, :] * jnp.concatenate([scale] * 4, axis=1)
            out_rows = [jnp.concatenate([values[at + 2 * r : at + 2 * r + 1] for r in range(4)], axis=0) for at in (0, 1, 8, 9)]
            for i in range(2):
                out_ref[c, s + i] = out_rows[i].astype(BF16)
                outbox[s + i] = out_rows[2 + i].astype(BF16)
            pair = pl.ds(s, 2)
            pltpu.make_async_remote_copy(
                src_ref=outbox.at[pair],
                dst_ref=out_ref.at[c, pair],
                send_sem=out_send,
                recv_sem=out_recv,
                device_id=(mate, d),
                device_id_type=MESH,
            ).start()
            return carry

        lax.fori_loop(0, many, one, 0)

    def place(slot):
        h, n = slot // 16, (slot + 15) % 16
        dx, dy = place_of(h, n)
        return h, (4 - dx) % 4, (4 - dy) % 4

    def arrive(slot, carry):
        h, dx, dy = place(slot)
        bx, by = (xx + dx) % 4, (yy + dy) % 4

        @pl.when(slot % 16 > 0)
        def _():
            wait_for(panel.at[bx, by, h], plane_recv.at[h, bx, by])

        cross(slot, h, dx, dy)
        return carry

    lax.fori_loop(0, FIRST, arrive, 0)
    loads[3].wait()
    finish(0, FIRST, place)
    lax.fori_loop(FIRST, SECOND, arrive, 0)
    finish(FIRST, SECOND - FIRST, lambda n: place(n + FIRST))
    lax.fori_loop(SECOND, 32, arrive, 0)
    finish(SECOND, 32 - SECOND, lambda n: place(n + SECOND))

    @pl.when(is_holder)
    def _():
        wait_for(picks.at[pl.ds(0, 7)], unit_send)
        wait_for(picks.at[pl.ds(0, 11)], line_send)

    @pl.when(jnp.logical_not(is_holder))
    def _():
        wait_for(picks.at[pl.ds(0, 8)], unit_send)

    @pl.when(is_relay)
    def _():
        wait_for(panel.at[0, pl.ds(0, 2)], relay_send)

    to_mate.wait_send()
    for part in range(3):
        wait_for(panel.at[part], plane_send)
    wait_for(panel.at[3, pl.ds(0, 3)], plane_send)
    wait_for(outbox, out_send)
    wait_for(outbox, out_recv)


def on_device(records, usable, panel_ids):
    vmem = pl.BlockSpec(memory_space=pltpu.VMEM)
    dma = pltpu.SemaphoreType.DMA
    return pl.pallas_call(
        kernel,
        out_shape=jax.ShapeDtypeStruct((2, 64, 4, NLAG), BF16),
        in_specs=[pl.BlockSpec(memory_space=pltpu.SMEM)] + [pl.BlockSpec(memory_space=pltpu.HBM)] * 3,
        out_specs=vmem,
        scratch_shapes=[
            pltpu.VMEM((4, 4, 2048), BF16),
            pltpu.VMEM((4, 2048), jnp.int32),
            pltpu.VMEM((896, 512), BF16),
            pltpu.VMEM((8, 2, 16, 128), BF16),
            pltpu.VMEM((16, 2, 16, 128), BF16),
            pltpu.VMEM((4, 4, 2, 8, 16, 128), BF16),
            pltpu.VMEM((16, 16, 128), BF16),
            pltpu.VMEM((16, 16, 128), BF16),
            pltpu.VMEM((2, 16, 4, 8, 128), F32),
            pltpu.VMEM((512, 2048), BF16),
            pltpu.VMEM((320, NLAG), F32),
            pltpu.VMEM((2048, NLAG), BF16),
            pltpu.VMEM((512, 128), F32),
            pltpu.VMEM((64, 4, NLAG), BF16),
            dma((4,)),
            dma,
            dma,
            dma,
            dma,
            dma,
            dma((2,)),
            dma,
            dma,
            dma((2, 4, 4)),
            dma,
            dma,
        ],
        compiler_params=pltpu.CompilerParams(
            collective_id=0, has_side_effects=True, vmem_limit_bytes=52 * 1024 * 1024
        ),
    )(*[pltpu.with_memory_space_constraint(a, pltpu.HBM) for a in (panel_ids, records, usable.T, jnp.asarray(make_tables()))])


def solution(mesh):
    return jax.shard_map(
        on_device,
        mesh=mesh,
        in_specs=(P(("grp", "dev"), None, None), P(), P()),
        out_specs=P(None, None, ("grp", "dev"), None),
        check_vma=False,
    )
```

```python
import math

import jax
import jax.numpy as jnp
import ml_dtypes
import numpy as np
from jax import lax
from jax.experimental import pallas as pl
from jax.experimental.pallas import tpu as pltpu
from jax.sharding import PartitionSpec as P

L = 2048
NF = 1024
RADIUS = 64
NLAG = 512
F32 = jnp.float32
BF16 = jnp.bfloat16
MESH = pl.DeviceIdType.MESH


def bins_of():
    lane = np.arange(128)
    bins = np.zeros((8, 128), np.int64)
    bins[0] = np.where(lane < 64, 16 * lane + 8, 16 * (lane - 63))
    for r in range(1, 8):
        bins[r] = 16 * lane + r
    return bins


def split_table(table):
    high = table.astype(ml_dtypes.bfloat16)
    low = (table - high.astype(np.float64)).astype(ml_dtypes.bfloat16)
    return high, low


def make_tables():
    bins = bins_of()
    natural = np.where(bins > NF, L - bins, bins)
    b = np.arange(128)
    angle = 2 * np.pi * np.outer(b, b) / 128
    cos, sin = np.cos(angle), np.sin(angle)
    dft = np.block([[cos, -sin], [sin, cos]])
    special = np.zeros((384, 256))
    for lane in range(64):
        special[128:256, lane] = cos[:, lane]
        special[256:384, lane] = sin[:, lane]
        special[128:256, 128 + lane] = -sin[:, lane]
        special[256:384, 128 + lane] = cos[:, lane]
    for lane in range(64, 128):
        special[0:128, lane] = np.cos(2 * np.pi * b * (lane - 63) / 128)
        special[0:128, 128 + lane] = -np.sin(2 * np.pi * b * (lane - 63) / 128)
    r = np.arange(16)[:, None]
    twiddle = 2 * np.pi * r * b[None, :] / L
    turn = np.concatenate([np.cos(twiddle), np.sin(twiddle)])

    def near(left, right):
        return (np.abs(natural[left][:, None] - natural[right][None, :]) <= RADIUS).astype(np.float64)

    band = np.concatenate([near(1, 2), near(2, 2), near(3, 2), near(0, 2)], axis=0)
    band0 = np.concatenate([near(1, 0), near(0, 0)], axis=0)
    lag = np.arange(NLAG) - NLAG // 2
    phase = 2 * np.pi * ((bins.reshape(-1)[:, None] * lag[None, :]) % L) / L
    ltable = np.concatenate([np.cos(phase), -np.sin(phase)], axis=0) / math.sqrt(NF)
    bf = ml_dtypes.bfloat16
    turns = np.zeros((128, 256), bf)
    turns[:32, :128], turns[:32, 128:] = split_table(turn)
    rows = [
        ltable.astype(bf),
        np.concatenate(split_table(special), axis=1),
        np.concatenate(split_table(dft), axis=1),
        np.concatenate([band[128 * n : 128 * n + 128] for n in range(4)], axis=1).astype(bf),
        np.concatenate([band0[:128].astype(bf), band0[128:].astype(bf), turns], axis=1),
    ]
    return np.concatenate(rows, axis=0)


def split(values):
    high = values.astype(BF16)
    return high, (values - high.astype(F32)).astype(BF16)


def dot(left, right):
    return jnp.dot(left, right, preferred_element_type=F32)


def transform(rows, tab_ref):
    count = rows.shape[0]
    x = [rows[:, 128 * a : 128 * a + 128] for a in range(16)]
    even = [None] + [x[a] + x[16 - a] for a in range(1, 8)]
    odd = [None] + [x[a] - x[16 - a] for a in range(1, 8)]
    parts_re, parts_im = [], []
    for r in range(9):
        re = x[0] + x[8] if r % 2 == 0 else x[0] - x[8]
        im = None
        for a in range(1, 8):
            c = math.cos(2 * math.pi * ((a * r) % 16) / 16)
            s = math.sin(2 * math.pi * ((a * r) % 16) / 16)
            if abs(c) > 1e-9:
                re = re + even[a] * c
            if abs(s) > 1e-9:
                im = odd[a] * -s if im is None else im + odd[a] * -s
        parts_re.append(re)
        parts_im.append(im)
    turn = tab_ref[768:800, 256:384].astype(F32) + tab_ref[768:800, 384:512].astype(F32)
    turned = []
    for r in range(1, 8):
        c, s = turn[r : r + 1], turn[16 + r : 17 + r]
        turned.append(jnp.concatenate([parts_re[r] * c + parts_im[r] * s, parts_im[r] * c - parts_re[r] * s], axis=1))
    y = jnp.concatenate(turned, axis=0)
    c, s = turn[8:9], turn[24:25]
    y0 = jnp.concatenate([parts_re[0], parts_re[8] * c, -(parts_re[8] * s)], axis=1)

    def product(values, at):
        high, low = split(values)
        n, depth = values.shape
        both = dot(jnp.concatenate([high, low], axis=0), tab_ref[at : at + depth, :256])
        return both[:n] + both[n:] + dot(high, tab_ref[at : at + depth, 256:])

    spectra = product(y, 384)
    spectra0 = product(y0, 0)
    re = [spectra0[:, :128]] + [spectra[count * j : count * j + count, :128] for j in range(7)]
    im = [spectra0[:, 128:]] + [spectra[count * j : count * j + count, 128:] for j in range(7)]
    return re, im


def running_mean(amplitude, tab_ref):
    count = amplitude[0].shape[0]
    below = [None, jnp.zeros_like(amplitude[0])]
    for r in range(2, 9):
        below.append(below[r - 1] + amplitude[r - 1])
    total = below[8]
    left = jnp.concatenate(
        [
            jnp.concatenate([below[r], amplitude[r], total - below[r] - amplitude[r], amplitude[0]], axis=1)
            for r in range(1, 8)
        ],
        axis=0,
    )
    left0 = jnp.concatenate([total, amplitude[0]], axis=1)

    def product(values, at):
        both = jnp.concatenate(split(values), axis=0)
        n = values.shape[0]
        sums = dot(both[:, :128], tab_ref[at : at + 128, :128])
        for k in range(1, values.shape[1] // 128):
            piece = slice(128 * k, 128 * k + 128)
            sums = sums + dot(both[:, piece], tab_ref[at : at + 128, piece])
        return sums[:n] + sums[n:]

    sums = product(left, 640)
    sums0 = product(left0, 768)
    scale = 1.0 / (2 * RADIUS + 1)
    return [sums0 * scale] + [sums[count * j : count * j + count] * scale for j in range(7)]


def kernel(
    panel_ids_ref,
    x_hbm,
    usable_hbm,
    tables_hbm,
    out_ref,
    x_ref,
    usable_ref,
    tab_ref,
    units,
    picks,
    panel,
    own,
    other,
    recv,
    lhs,
    lagged,
    lt_ref,
    scales,
    outbox,
    in_sem,
    unit_send,
    unit_recv,
    other_send,
    other_recv,
    line_send,
    line_recv,
    relay_send,
    plane_send,
    plane_recv,
    out_send,
    out_recv,
):
    g = lax.axis_index("grp")
    d = lax.axis_index("dev")
    z_lo, c = g // 2, g % 2
    z_hi, xx, yy = d // 16, (d // 4) % 4, d % 4
    mate = z_lo * 2 + (1 - c)

    loads = [
        pltpu.make_async_copy(source, target, in_sem.at[n])
        for n, (source, target) in enumerate(
            [
                (x_hbm, x_ref),
                (tables_hbm.at[pl.ds(2048, 896)], tab_ref),
                (usable_hbm, usable_ref),
                (tables_hbm.at[pl.ds(0, 2048)], lt_ref),
            ]
        )
    ]
    for load in loads:
        load.start()

    barrier = pltpu.get_barrier_semaphore()

    def hello(grp, dev):
        pl.semaphore_signal(barrier, inc=1, device_id=(grp, dev), device_id_type=MESH)

    held = 1 - (z_lo // 4 - z_hi) * (z_lo // 4 - z_hi)
    quad = z_lo % 4
    is_holder = held == 1

    def holder_chip(side, n):
        return side * (7 - n) + (1 - side) * n

    zz = z_hi * 8 + z_lo
    is_far = z_hi * (1 - z_lo // 4) == 1
    is_relay = (zz - 7) * (zz - 12) == 0

    def line_device(z):
        return (z % 8) * 2 + c, (z // 8) * 16 + d % 16

    def hello_holder(n, carry):
        side = n // 4
        z = side * 8 + holder_chip(side, n % 4)

        @pl.when(z != zz)
        def _():
            hello(*line_device(z))

        return carry

    @pl.when(jnp.logical_not(is_far))
    def _():
        lax.fori_loop(0, 8, hello_holder, 0)

    @pl.when(is_far)
    def _():
        hello(*line_device(7 + 5 * ((zz - 8) // 2)))

    def hello_grp(n, carry):
        hello((g + n) % 16, d)
        return carry

    @pl.when(is_holder)
    def _():
        lax.fori_loop(1, 16, hello_grp, 0)

    @pl.when(jnp.logical_not(is_holder))
    def _():
        hello(mate, d)

    def hello_plane(k, carry):
        hello(g, z_hi * 16 + ((xx + k) % 4) * 4 + yy)
        hello(g, z_hi * 16 + xx * 4 + (yy + k) % 4)
        return carry

    lax.fori_loop(1, 4, hello_plane, 0)

    for load in loads[:3]:
        load.wait()
    loaded = [x_ref[ch].astype(F32) for ch in range(4)]
    rows = jnp.concatenate(
        [loaded[2 * pair + i][w : w + 1] for pair in range(2) for w in range(4) for i in range(2)], axis=0
    )
    spec_re, spec_im = transform(rows, tab_ref)
    amplitude = [jnp.sqrt(re * re + im * im) for re, im in zip(spec_re, spec_im)]
    smooth = running_mean(amplitude, tab_ref)

    lane16 = lax.broadcasted_iota(jnp.int32, (16, 128), 1)
    row16 = lax.broadcasted_iota(jnp.int32, (16, 128), 0)

    def twice(block):
        return jnp.concatenate([block[w // 2 : w // 2 + 1] for w in range(8)], axis=0)

    def mask_of(group):
        block = usable_ref[:, pl.ds(pl.multiple_of(group * 128, 128), 128)].astype(F32)
        tiled = jnp.concatenate([twice(block)] * 2, axis=0)
        chosen = jnp.where(lane16 == 4 * d + (row16 // 8) * 2 + row16 % 2, tiled, 0.0)
        return jnp.sum(chosen, axis=1, keepdims=True)

    own_mask = mask_of(g)
    mate_mask = mask_of(mate)

    upper = [(jnp.full((8, 128), panel_ids_ref[t]) & 1) == 1 for t in range(2)]
    for k in range(8):
        inverse = 1.0 / (smooth[k] + 1e-06)
        re = (spec_re[k] * inverse).astype(BF16).astype(F32) * own_mask
        im = (spec_im[k] * inverse).astype(BF16).astype(F32) * own_mask
        own[k] = re.astype(BF16)
        own[8 + k] = im.astype(BF16)
        for t in range(2):
            pair = jnp.concatenate(
                [jnp.where(upper[t], re[8:], re[:8]), jnp.where(upper[t], im[8:], im[:8])], axis=0
            )
            units[(k // 2) * 2 + t, k % 2] = pair.astype(BF16)

    @pl.when(is_relay)
    def _():
        pl.semaphore_wait(barrier, 17 + 9 * held)

    @pl.when(jnp.logical_not(is_relay))
    def _():
        pl.semaphore_wait(barrier, 15 + 9 * held)


    def send_unit(n, carry):
        chip = holder_chip(z_hi, n // 2)
        to = chip * 2 + n % 2

        @pl.when(to != g)
        def _():
            pltpu.make_async_remote_copy(
                src_ref=units.at[(chip % 4) * 2 + n % 2],
                dst_ref=picks.at[g],
                send_sem=unit_send,
                recv_sem=unit_recv,
                device_id=(to, d),
                device_id_type=MESH,
            ).start()

        return carry

    lax.fori_loop(0, 8, send_unit, 0)
    to_mate = pltpu.make_async_remote_copy(
        src_ref=own,
        dst_ref=other,
        send_sem=other_send,
        recv_sem=other_recv,
        device_id=(mate, d),
        device_id_type=MESH,
    )
    to_mate.start()
    chosen = panel_ids_ref[c]
    owner = jnp.full((16, 128), chosen) >> 1

    sub = lax.broadcasted_iota(jnp.int32, (8, 128), 0)
    first_of_pair = sub % 2 == 0

    def spread(side, source):
        def one(p, carry):
            tile = source[p].astype(F32)
            for pair in range(2):
                rows8 = tile[8 * pair : 8 * pair + 8]
                recv[side, p, 2 * pair] = jnp.where(first_of_pair, rows8, pltpu.roll(rows8, 1, 0))
                recv[side, p, 2 * pair + 1] = jnp.where(first_of_pair, pltpu.roll(rows8, 7, 0), rows8)
            return carry

        lax.fori_loop(0, 16, one, 0)

    spread(0, own)
    to_mate.wait_recv()
    spread(1, other)

    block = usable_ref[:, :128]
    for k in range(1, 16):
        block = jnp.where(owner[:4] == k, usable_ref[:, 128 * k : 128 * k + 128], block)
    block = block.astype(F32)
    weights = jnp.concatenate([twice(block)] * 4, axis=0) * jnp.concatenate([own_mask, mate_mask], axis=0)
    row = lax.broadcasted_iota(jnp.int32, (512, 128), 0)
    lane = lax.broadcasted_iota(jnp.int32, (512, 128), 1)
    at_x = (xx + row // 128) % 4
    at_y = (yy + (row // 32) % 4) % 4
    at_dev = ((row // 16) % 2) * 16 + at_x * 4 + at_y
    half = jnp.full((512, 128), chosen) & 1
    picked = jnp.where(lane == at_dev * 4 + half * 2 + row % 2, 1.0, 0.0).astype(BF16)
    counts = lax.dot_general(picked, weights.astype(BF16), (((1,), (1,)), ((), ())), preferred_element_type=F32)
    row32 = lax.broadcasted_iota(jnp.int32, (512, 32), 0)
    lane32 = lax.broadcasted_iota(jnp.int32, (512, 32), 1)
    match = (lane32 // 8) * 2 + lane32 % 2 == ((row32 // 8) % 2) * 4 + (row32 // 2) % 4
    count = jnp.sum(jnp.where(match, counts, 0.0), axis=1, keepdims=True)
    scales[...] = jnp.broadcast_to(1.0 / jnp.maximum(count, 1.0), (512, 128))

    def wait_for(ref, sem):
        pltpu.make_async_copy(ref, ref, sem).wait()

    mine = panel.at[xx, yy, z_hi, pl.ds(2 * quad, 2)]

    def send_line(n, carry):
        z = (n // 2) * (1 - n % 2) + (15 - n // 2) * (n % 2)
        z = z - 4 * ((n // 8) * (n % 2))

        @pl.when(z != zz)
        def _():
            pltpu.make_async_remote_copy(
                src_ref=mine,
                dst_ref=mine,
                send_sem=line_send,
                recv_sem=line_recv.at[z_hi],
                device_id=line_device(z),
                device_id_type=MESH,
            ).start()

        return carry

    @pl.when(is_holder)
    def _():
        picks[g] = units[quad * 2 + c]
        wait_for(picks.at[pl.ds(0, 15)], unit_recv)
        for b in range(2):
            pick = jnp.where(owner == 0, picks[0, b].astype(F32), 0.0)
            for k in range(1, 16):
                pick = jnp.where(owner == k, picks[k, b].astype(F32), pick)
            panel[xx, yy, z_hi, 2 * quad + b] = pick.astype(BF16)
        lax.fori_loop(0, 12, send_line, 0)

    def wait_line(h):
        missing = held * (1 - (z_hi - h) * (z_hi - h))

        @pl.when(missing == 1)
        def _():
            wait_for(panel.at[0, 0, 0, pl.ds(0, 6)], line_recv.at[h])

        @pl.when(missing == 0)
        def _():
            wait_for(panel.at[0, 0, 0], line_recv.at[h])

        def relay(n, carry):
            ref = panel.at[xx, yy, h]
            pltpu.make_async_remote_copy(
                src_ref=ref,
                dst_ref=ref,
                send_sem=relay_send,
                recv_sem=line_recv.at[h],
                device_id=line_device(8 + n + z_hi * (3 - 2 * n)),
                device_id_type=MESH,
            ).start()
            return carry

        @pl.when(is_relay)
        def _():
            lax.fori_loop(0, 2, relay, 0)

    def send_block(h, u, bx, by, tx, ty):
        ref = panel.at[bx, by, h, pl.ds(4 * u, 4)]
        pltpu.make_async_remote_copy(
            src_ref=ref,
            dst_ref=ref,
            send_sem=plane_send,
            recv_sem=plane_recv.at[h, u, bx, by],
            device_id=(g, z_hi * 16 + tx * 4 + ty),
            device_id_type=MESH,
        ).start()

    def wait_block(h, u, bx, by):
        wait_for(panel.at[bx, by, h, pl.ds(4 * u, 4)], plane_recv.at[h, u, bx, by])

    def distance(n):
        return 1 + 2 * (n % 2) + n // 2

    def others(n, own_place):
        return n + (n + 4 - own_place) // 4

    def to_x(h):
        def send(n, carry):
            send_block(h, n // 3, xx, yy, others(n % 3, xx), yy)
            return carry

        lax.fori_loop(0, 6, send, 0)

    def to_y(h):
        def send(n, carry):
            send_block(h, n // 3, xx, yy, xx, others(n % 3, yy))
            return carry

        lax.fori_loop(0, 6, send, 0)

    wait_line(0)
    to_x(0)
    wait_line(1)
    to_y(1)
    to_y(0)
    to_x(1)

    def forward(n, carry):
        u, k = n % 2, distance(n // 2)
        bx, by = (xx + k) % 4, (yy + k) % 4
        wait_block(0, u, bx, yy)

        def on_y(m, inner):
            send_block(0, u, bx, yy, xx, others(m, yy))
            return inner

        lax.fori_loop(0, 3, on_y, 0)
        wait_block(1, u, xx, by)

        def on_x(m, inner):
            send_block(1, u, xx, by, others(m, xx), yy)
            return inner

        lax.fori_loop(0, 3, on_x, 0)
        return carry

    window = sub // 2
    lower = window < 2
    inner_two = (window == 1) | (window == 2)
    even = window % 2 == 0

    def fold(v):
        u = jnp.where(lower, v[0], v[2]) + pltpu.roll(jnp.where(lower, v[2], v[0]), 4, 0)
        t = jnp.where(inner_two, v[1], v[3]) + pltpu.roll(jnp.where(inner_two, v[3], v[1]), 4, 0)
        return jnp.where(even, u, t) + pltpu.roll(jnp.where(even, t, u), 6, 0)

    def cross(slot, h, dx, dy):
        bx, by = (xx + dx) % 4, (yy + dy) % 4
        at = pl.ds(pl.multiple_of(slot * 16, 16), 16)
        for k in range(8):
            both = panel[bx, by, h, k].astype(F32)
            a, b = both[:8], both[8:]
            re_rows, im_rows = [], []
            for side in range(2):
                re, im = [], []
                for r in range(4):
                    cc, ee = recv[side, k, r], recv[side, 8 + k, r]
                    re.append(a * cc + b * ee)
                    im.append(b * cc - a * ee)
                re_rows.append(fold(re))
                im_rows.append(fold(im))
            lhs[at, 128 * k : 128 * k + 128] = jnp.concatenate(re_rows, axis=0).astype(BF16)
            lhs[at, 1024 + 128 * k : 1152 + 128 * k] = jnp.concatenate(im_rows, axis=0).astype(BF16)

    def finish(first, many, place):
        rows = pl.ds(pl.multiple_of(first * 16, 16), many * 16)
        lagged[: many * 16] = dot(lhs[rows, :], lt_ref[...])

        def one(n, carry):
            h, dx, dy = place(n)
            s = (h * 16 + ((xx + dx) % 4) * 4 + (yy + dy) % 4) * 2
            scale = scales[pl.ds(pl.multiple_of((dx * 8 + dy * 2 + h) * 16, 16), 16), :]
            slot_rows = pl.ds(pl.multiple_of(n * 16, 16), 16)
            values = lagged[slot_rows, :] * jnp.concatenate([scale] * 4, axis=1)
            out_rows = [jnp.concatenate([values[at + 2 * r : at + 2 * r + 1] for r in range(4)], axis=0) for at in (0, 1, 8, 9)]
            for i in range(2):
                out_ref[c, s + i] = out_rows[i].astype(BF16)
                outbox[s + i] = out_rows[2 + i].astype(BF16)
            pair = pl.ds(s, 2)
            pltpu.make_async_remote_copy(
                src_ref=outbox.at[pair],
                dst_ref=out_ref.at[c, pair],
                send_sem=out_send,
                recv_sem=out_recv,
                device_id=(mate, d),
                device_id_type=MESH,
            ).start()
            return carry

        lax.fori_loop(0, many, one, 0)

    def first_place(n):
        k, axis, h = distance(n // 4), (n // 2) % 2, n % 2
        return h, k * (1 - axis), k * axis

    def cross_own(h, carry):
        cross(h, h, 0, 0)
        return carry

    lax.fori_loop(0, 2, cross_own, 0)

    def cross_first(n, carry):
        h, dx, dy = first_place(n)

        @pl.when(dx * (1 - h) + dy * h == 0)
        def _():
            wait_block(h, 0, (xx + dx) % 4, (yy + dy) % 4)
            wait_block(h, 1, (xx + dx) % 4, (yy + dy) % 4)

        cross(n + 2, h, dx, dy)
        return carry

    def forward_and_cross(n, carry):
        forward(n, carry)

        @pl.when(n % 2 == 1)
        def _():
            lax.fori_loop(0, 2, lambda m, inner: cross_first(4 * (n // 2) + 3 * m, inner), 0)

        return carry

    lax.fori_loop(0, 6, forward_and_cross, 0)
    lax.fori_loop(0, 6, lambda n, inner: cross_first(4 * (n // 2) + 1 + n % 2, inner), 0)
    loads[3].wait()

    def early_place(n):
        h, dx, dy = first_place(n - 2 * jnp.minimum(n // 2, 1))
        later = jnp.minimum(n // 2, 1)
        return h, dx * later, dy * later

    finish(0, 14, early_place)

    def second_place(n):
        k, m, h = distance(n // 6), distance((n // 2) % 3), n % 2
        return h, k * (1 - h) + m * h, m * (1 - h) + k * h

    def cross_second(n, carry):
        h, dx, dy = second_place(n)
        wait_block(h, 0, (xx + dx) % 4, (yy + dy) % 4)
        wait_block(h, 1, (xx + dx) % 4, (yy + dy) % 4)
        cross(14 + n, h, dx, dy)
        return carry

    lax.fori_loop(0, 18, cross_second, 0)
    finish(14, 18, second_place)

    @pl.when(is_holder)
    def _():
        wait_for(picks.at[pl.ds(0, 7)], unit_send)
        wait_for(picks.at[pl.ds(0, 11)], line_send)

    @pl.when(jnp.logical_not(is_holder))
    def _():
        wait_for(picks.at[pl.ds(0, 8)], unit_send)

    @pl.when(is_relay)
    def _():
        wait_for(panel.at[0, pl.ds(0, 2)], relay_send)

    to_mate.wait_send()
    for part in range(3):
        wait_for(panel.at[part], plane_send)
    wait_for(panel.at[3, pl.ds(0, 3)], plane_send)
    wait_for(outbox, out_send)
    wait_for(outbox, out_recv)


def on_device(records, usable, panel_ids):
    vmem = pl.BlockSpec(memory_space=pltpu.VMEM)
    dma = pltpu.SemaphoreType.DMA
    return pl.pallas_call(
        kernel,
        out_shape=jax.ShapeDtypeStruct((2, 64, 4, NLAG), BF16),
        in_specs=[pl.BlockSpec(memory_space=pltpu.SMEM)] + [pl.BlockSpec(memory_space=pltpu.HBM)] * 3,
        out_specs=vmem,
        scratch_shapes=[
            pltpu.VMEM((4, 4, 2048), BF16),
            pltpu.VMEM((4, 2048), jnp.int32),
            pltpu.VMEM((896, 512), BF16),
            pltpu.VMEM((8, 2, 16, 128), BF16),
            pltpu.VMEM((16, 2, 16, 128), BF16),
            pltpu.VMEM((4, 4, 2, 8, 16, 128), BF16),
            pltpu.VMEM((16, 16, 128), BF16),
            pltpu.VMEM((16, 16, 128), BF16),
            pltpu.VMEM((2, 16, 4, 8, 128), F32),
            pltpu.VMEM((512, 2048), BF16),
            pltpu.VMEM((288, NLAG), F32),
            pltpu.VMEM((2048, NLAG), BF16),
            pltpu.VMEM((512, 128), F32),
            pltpu.VMEM((64, 4, NLAG), BF16),
            dma((4,)),
            dma,
            dma,
            dma,
            dma,
            dma,
            dma((2,)),
            dma,
            dma,
            dma((2, 2, 4, 4)),
            dma,
            dma,
        ],
        compiler_params=pltpu.CompilerParams(
            collective_id=0, has_side_effects=True, vmem_limit_bytes=52 * 1024 * 1024
        ),
    )(*[pltpu.with_memory_space_constraint(a, pltpu.HBM) for a in (panel_ids, records, usable.T, jnp.asarray(make_tables()))])


def solution(mesh):
    return jax.shard_map(
        on_device,
        mesh=mesh,
        in_specs=(P(("grp", "dev"), None, None), P(), P()),
        out_specs=P(None, None, ("grp", "dev"), None),
        check_vma=False,
    )
```
